512 devices in a mesh: section: 16 (over x_lo, z), latent: 32 (over x_hi, y, core).
Axes of the slice: x: 4 (x_hi: 2, x_lo: 2; x = x_hi * 2 + x_lo), y: 8, z: 8, core: 2. Of those that a mesh axis runs over, the one named last changes fastest.
Arguments:
- residual: bfloat16 [4, 320, 4608], P(None, None, 'latent'), may hold values from -6 to 6
- encoder: bfloat16 [16, 4608, 4096], P('section', None, 'latent'), may hold values from -0.09375 to 0.09375
- enc_bias: float32 [16, 4096], P('section', 'latent'), may hold values from -4 to 4
- gate_code: int32 [16, 4096], P('section', 'latent'), may hold values from 0 to 2
- decoder: bfloat16 [16, 3, 4096, 4608], P('section', None, 'latent'), may hold values from -0.0546875 to 0.0546875
Outputs:
- reconstruction: bfloat16 [16, 80, 4608], P('section', None, 'latent')
- latent_acts: bfloat16 [16, 320, 4096], P('section', None, 'latent')
The draws below stay inside these ranges and needn't reach their ends.
Inputs may be any that keep to these rules, and one draw needn't show every extreme that they name: `gate_code`: 0: the latent is always active; 1: its threshold is zero; 2: it is never active.
All inputs are finite; a program needn't handle non-finite values.
Results may differ from the reference program's by a relative error of at most 0.019.
Values may be sent and summed in bfloat16 or wider, within the bound.
A program may use at most 64 MiB of HBM per device.

```python
import jax
import jax.numpy as jnp
from jax import lax

D = 4608
LAYERS = 4
LAT_DEV = 128
REACH = 3
TOK = 320
GROUP = 4
LATG = 4096
LATENTS = 16384
N_SECTION = 16
N_LATENT = 32


def with_ends(drawn, own_key, least, high):
    longest = drawn.shape.index(max(drawn.shape))
    spots = []
    for shift in (0, 1):
        where = [jax.random.randint(jax.random.fold_in(own_key, axis), (), 0, length) for axis, length in enumerate(drawn.shape)]
        where[longest] = (where[longest] + shift) % drawn.shape[longest]
        spots.append(tuple(where))
    return drawn.at[spots[0]].set(least).at[spots[1]].set(high)


def strengthened(array, stream_key, source, target, blocks, factor):
    owner, partner = [(jnp.arange(array.shape[position]) // (array.shape[position] // blocks)).reshape([-1 if axis == position else 1 for axis in range(array.ndim)]) for position in (source, target)]
    chosen = jax.random.permutation(stream_key, blocks)[partner]
    strong = (owner == chosen) | (owner == (partner + blocks // 2) % blocks)
    return jnp.where(strong, factor * array, array)


def level_of(rng, dims, split, low, largest):
    def one(position, blocks):
        heights = jax.random.uniform(jax.random.fold_in(jax.random.fold_in(rng, 6), position), (blocks,), jnp.float32, low / len(split), largest / len(split))
        return jnp.repeat(jnp.exp(heights), dims[position] // blocks).reshape((-1,) + (1,) * (len(dims) - position - 1))

    level = one(*split[0])
    for cut in split[1:]:
        level = level * one(*cut)
    return level


def centred(key, dims, scale, limit, split=(), held_as=jnp.bfloat16):
    values = jax.random.normal(key, dims, jnp.float32) * scale
    if len(split) > 0:
        values = level_of(key, dims, split, -0.22, 0.18) * values
    return jnp.clip(values, min=-limit, max=limit).astype(held_as)


def gaussian_with(rng, dims, scale, reach, shards, heavy, held_as=jnp.bfloat16):
    entries = scale * jax.random.normal(rng, dims, jnp.float32)
    if shards:
        entries = entries * level_of(rng, dims, shards, -0.22, 0.18)
    return jnp.clip(strengthened(entries, jax.random.fold_in(rng, 3), *heavy), -reach, reach).astype(held_as)


def setup_inputs(seed: int = 0) -> dict:
    keys = jax.random.split(jax.random.key(seed), 6)
    residual = centred(keys[0], (LAYERS, TOK, D), 1.0, 6.0, ((2, 32),))
    encoder = centred(keys[1], (N_SECTION, D, LATG), D ** -0.5, 0.09375, ((0, 16), (2, 32)))
    enc_bias = centred(keys[2], (N_SECTION, LATG), 1.0, 4.0, ((0, 16), (1, 32)), jnp.float32)
    gate_code = with_ends(jax.random.randint(keys[3], (N_SECTION, LATG), 0, 3), jax.random.fold_in(keys[3], 1), 0, 2).astype(jnp.int32)
    decoder = gaussian_with(keys[4], (N_SECTION, REACH, LATG, D), (LATENTS * REACH) ** -0.5, 0.0546875, ((0, 16), (2, 32)), (2, 3, 32, 2.75))
    return {"residual": residual, "encoder": encoder, "enc_bias": enc_bias, "gate_code": gate_code, "decoder": decoder}


def reference(residual, encoder, enc_bias, gate_code, decoder):
    threshold = 10000.0 * (gate_code.astype(jnp.float32) - 1.0)
    resid_rows = jnp.repeat(residual, GROUP, axis=0)

    def encode(inputs):
        resid_layer, enc_layer, bias_layer, thresh_layer = inputs
        preact = jnp.dot(resid_layer, enc_layer, preferred_element_type=jnp.float32) + bias_layer
        return jnp.where(preact > thresh_layer, preact, jnp.zeros_like(preact)).astype(jnp.bfloat16)

    latent_acts = lax.map(encode, (resid_rows, encoder, enc_bias, threshold))
    slots = LAYERS * GROUP
    shifted = []
    for hop_index in range(REACH):
        lead = hop_index * GROUP
        zero_start = jnp.zeros((lead, TOK, LATG), jnp.bfloat16)
        shifted.append(jnp.concatenate([zero_start, latent_acts[:slots - lead]], axis=0))
    sources = jnp.stack(shifted, axis=1)

    def decode(inputs):
        source_acts, dec_layer = inputs
        spread = source_acts.astype(jnp.float32).reshape(REACH, TOK, N_LATENT, LAT_DEV)
        weights_full = dec_layer.astype(jnp.float32).reshape(REACH, N_LATENT, LAT_DEV, D)
        shares = jnp.einsum("ktjl,kjld->jtd", spread, weights_full, precision=lax.Precision.HIGHEST)
        shares = lax.optimization_barrier(shares.astype(jnp.bfloat16)).astype(jnp.float32)
        return jnp.sum(shares, axis=0)

    parts_all = lax.map(decode, (sources, decoder))
    full = jnp.sum(parts_all.reshape(LAYERS, GROUP, TOK, D), axis=1).astype(jnp.bfloat16)
    reconstruction = full.reshape(LAYERS * GROUP, TOK // GROUP, D)
    return reconstruction, latent_acts
```

```python
import jax
import jax.numpy as jnp
from jax import lax
from jax.experimental import pallas as pl
from jax.experimental.pallas import tpu as pltpu
from jax.sharding import PartitionSpec as P

MESH = pl.DeviceIdType.MESH
BF16 = jnp.bfloat16
F32 = jnp.float32

NY = 8
GROUP = 4
OFFSETS = (4, 3, -3, 2, -2, 1, -1, 0)
PLACE = {offset: place for place, offset in enumerate(OFFSETS)}
PLACE[-4] = PLACE[4]


def kernel(
    resid, enc, bias, gate, dec, rec_out, act_out,
    gathered, enc_v, dec_v, enc_t, dec_t, acts_in, acts_all, shares, sibling_in, ring, own_sum, final_out, final_in,
    load_sem, local_sem, cross_send, cross_recv, gather_send, gather_recv, pair_send, pair_recv,
    act_send, act_recv, share_send, share_recv, ring_send, ring_recv, final_send, final_recv,
):
    width, tokens = gathered.shape[3:]
    section = lax.axis_index("section")
    latent = lax.axis_index("latent")
    x_lo, z = section // 8, section % 8
    x_hi, y, core = latent // 16, latent // 2 % 8, latent % 2
    layer, g = section // GROUP, section % GROUP

    def device(section_index, hi, y_index, core_index):
        return (section_index, hi * 16 + y_index * 2 + core_index)

    up = device(section, x_hi, (y + 1) % NY, core)
    down = device(section, x_hi, (y + NY - 1) % NY, core)
    sibling = device(section, x_hi, y, 1 - core)
    across = device((1 - x_lo) * 8 + z, 1 - x_hi, y, core)
    later = [((section + 4) % 16, latent), ((section + 8) % 16, latent)]
    peers = []
    for code in range(1, 8):
        flip_x, flip_g = code // 4, code % 4
        hi = 1 - x_hi if flip_x else x_hi
        low, high = g % 2, g // 2
        low = 1 - low if flip_g % 2 else low
        high = 1 - high if flip_g // 2 else high
        peer_g = high * 2 + low
        peers.append((hi, peer_g, device(section - g + peer_g, hi, y, core)))

    partners = [up, down, sibling, across, later[0], later[1], ((section + 12) % 16, latent)]
    partners += [peer[2] for peer in peers]
    barrier = pltpu.get_barrier_semaphore()
    for partner in partners:
        pl.semaphore_signal(barrier, inc=1, device_id=partner, device_id_type=MESH)
    loads = [
        pltpu.make_async_copy(enc, enc_v, load_sem.at[0]),
        pltpu.make_async_copy(dec, dec_v, load_sem.at[1]),
    ]
    for load in loads:
        load.start()
    local = pltpu.make_async_copy(resid.at[layer], gathered.at[x_hi, y, core], local_sem)
    local.start()
    local.wait()
    pl.semaphore_wait(barrier, len(partners))

    def remote(source, target, send, recv, to):
        copy = pltpu.make_async_remote_copy(
            src_ref=source, dst_ref=target, send_sem=send, recv_sem=recv, device_id=to, device_id_type=MESH
        )
        copy.start()
        return copy

    pending = []
    half = (x_hi, 1 - x_hi)
    crossed = remote(
        resid.at[(1 - x_lo) * 2 + z // 4], gathered.at[x_hi, y, core], cross_send, cross_recv, across
    )
    gather = {}
    pairs = {}

    def send_gather(step, way, q):
        origin = (y + (NY - step if way == 0 else step)) % NY
        block = gathered.at[half[q], origin, core]
        gather[step, way, q] = remote(
            block, block, gather_send.at[step, way, q], gather_recv.at[step, way, q], up if way == 0 else down
        )

    def send_pair(offset, q):
        origin = (y + (offset + NY) % NY) % NY
        block = gathered.at[half[q], origin, core]
        place = PLACE[offset]
        pairs[place, q] = remote(block, block, pair_send.at[place, q], pair_recv.at[place, q], sibling)

    for way in range(2):
        send_gather(0, way, 0)
    send_pair(0, 0)

    loads[0].wait()

    def turn_encoder(block, carry):
        rows = pl.ds(pl.multiple_of(block * 2 * width, 16), 2 * width)
        enc_t[block] = jnp.transpose(enc_v[0, rows, :])
        return carry

    lax.fori_loop(0, 16, turn_encoder, 0)
    crossed.wait_recv()
    for way in range(2):
        send_gather(0, way, 1)
    send_pair(0, 1)
    loads[1].wait()

    def turn_decoder(block, carry):
        columns = pl.ds(pl.multiple_of(block * 128, 128), 128)
        for k in range(3):
            dec_t[columns, k * 128 : (k + 1) * 128] = jnp.transpose(dec_v[0, k, :, columns])
        return carry

    lax.fori_loop(0, 36, turn_decoder, 0)

    def encoded(offset):
        origin = (y + (offset + NY) % NY) % NY
        for q in range(2):
            pairs[PLACE[offset], q].wait_recv()

        def one(hi, total):
            block = gathered[hi, origin].reshape(2 * width, tokens)
            return total + jnp.dot(enc_t[hi * NY + origin], block, preferred_element_type=F32)

        return lax.fori_loop(0, 2, one, jnp.zeros((128, tokens), F32))

    preact_t = None
    for step in range(4):
        for q in range(2):
            for way in range(2):
                if (step, way, q) not in gather:
                    continue
                gather[step, way, q].wait_recv()
                if step < 2 or (step == 2 and way == q):
                    send_gather(step + 1, way, q)
                send_pair((step + 1) * (-1 if way == 0 else 1), q)
        for offset in ((0,) if step == 0 else (step, -step)):
            term = encoded(offset)
            preact_t = term if preact_t is None else preact_t + term
    preact_t = preact_t + encoded(4)
    preact = jnp.transpose(preact_t) + bias[...]
    threshold = 10000.0 * (gate[...].astype(F32) - 1.0)
    acts = jnp.where(preact > threshold, preact, jnp.zeros_like(preact)).astype(BF16)
    act_out[0] = acts
    acts_all[:, 0:128] = acts
    passed = [
        remote(act_out.at[0], acts_in.at[k], act_send.at[k], act_recv.at[k], later[k]) for k in (1, 0)
    ][::-1]
    for k in (1, 0):
        passed[k].wait_recv()
        arrived = acts_in[k]
        acts_all[:, (k + 1) * 128 : (k + 2) * 128] = jnp.where(layer > k, arrived, jnp.zeros_like(arrived))

    share_copies = {}

    def decode(place):
        target = (y + (OFFSETS[place] + NY) % NY) % NY

        def one(hi, carry):
            rows = pl.ds(pl.multiple_of((hi * NY + target) * 2 * width, 16), 2 * width)
            product = lax.dot_general(
                dec_t[rows, :], acts_all[...], (((1,), (1,)), ((), ())), preferred_element_type=F32
            )
            shares[place, hi] = product.astype(BF16).reshape(2, width, tokens)
            return carry

        lax.fori_loop(0, 2, one, 0)
        for hi in range(2):
            share_copies[place, hi] = remote(
                shares.at[place, hi, 1 - core],
                sibling_in.at[place, hi],
                share_send.at[place, hi],
                share_recv.at[place, hi],
                sibling,
            )

    def chip_sum(place, hi):
        share_copies[place, hi].wait_recv()
        return shares[place, hi, core].astype(F32) + sibling_in[place, hi].astype(F32)

    ring_copies = {}

    def send_ring(way, distance, hi):
        ring_copies[way, distance, hi] = remote(
            ring.at[way, distance, hi],
            ring.at[way, distance - 1, hi],
            ring_send.at[way, distance, hi],
            ring_recv.at[way, distance, hi],
            up if way == 0 else down,
        )

    def add_ring(way, distance, hi):
        place = PLACE[distance if way == 0 else -distance]
        total = chip_sum(place, hi)
        if (way, distance + 1, hi) in ring_copies:
            ring_copies[way, distance + 1, hi].wait_recv()
            total = total + ring[way, distance, hi].astype(F32)
        ring[way, distance, hi] = total.astype(BF16)
        send_ring(way, distance, hi)

    decode(0)
    decode(1)
    for way in range(2):
        add_ring(way, 4, way)
    decode(2)
    for way in range(2):
        add_ring(way, 3, 1 - way)
    decode(3)
    decode(4)
    for way in range(2):
        add_ring(way, 3, way)
    decode(5)
    decode(6)
    for way in range(2):
        add_ring(way, 2, 1 - way)
    decode(7)
    for way in range(2):
        add_ring(way, 2, way)
    for hi in range(2):
        for way in range(2):
            add_ring(way, 1, hi if way == 1 else 1 - hi)
    for hi in range(2):
        total = chip_sum(7, hi)
        for way in range(2):
            ring_copies[way, 1, hi].wait_recv()
            total = total + ring[way, 0, hi].astype(F32)
        turned = jnp.transpose(total).reshape(GROUP, tokens // GROUP, width)
        own_sum[hi] = turned
        final_out[hi] = turned.astype(BF16)
    finals = [
        remote(final_out.at[hi, peer_g], final_in.at[i], final_send.at[i], final_recv.at[i], to)
        for i, (hi, peer_g, to) in enumerate(peers)
    ]
    total = own_sum[x_hi, g]
    for i, copy in enumerate(finals):
        copy.wait_recv()
        total = total + final_in[i].astype(F32)
    rec_out[0] = total.astype(BF16)

    for group in ([crossed], gather.values(), pairs.values(), passed, share_copies.values(), ring_copies.values(), finals):
        for copy in group:
            copy.wait_send()


def shards(residual, encoder, enc_bias, gate_code, decoder):
    layers, tokens, width = residual.shape
    model = encoder.shape[1]
    vmem = pl.BlockSpec(memory_space=pltpu.VMEM)
    hbm = pl.BlockSpec(memory_space=pl.ANY)
    dma = pltpu.SemaphoreType.DMA
    return pl.pallas_call(
        kernel,
        out_shape=(
            jax.ShapeDtypeStruct((1, tokens // GROUP, width), BF16),
            jax.ShapeDtypeStruct((1, tokens, 128), BF16),
        ),
        in_specs=[vmem, hbm, vmem, vmem, hbm],
        out_specs=(vmem, vmem),
        scratch_shapes=[
            pltpu.VMEM((2, NY, 2, width, tokens), BF16),
            pltpu.VMEM((1, model, 128), BF16),
            pltpu.VMEM((1, 3, 128, model), BF16),
            pltpu.VMEM((16, 128, 2 * width), BF16),
            pltpu.VMEM((model, 384), BF16),
            pltpu.VMEM((2, tokens, 128), BF16),
            pltpu.VMEM((tokens, 384), BF16),
            pltpu.VMEM((8, 2, 2, width, tokens), BF16),
            pltpu.VMEM((8, 2, width, tokens), BF16),
            pltpu.VMEM((2, 5, 2, width, tokens), BF16),
            pltpu.VMEM((2, GROUP, tokens // GROUP, width), F32),
            pltpu.VMEM((2, GROUP, tokens // GROUP, width), BF16),
            pltpu.VMEM((7, tokens // GROUP, width), BF16),
            dma((2,)),
            dma(()),
            dma(()),
            dma(()),
            dma((4, 2, 2)),
            dma((4, 2, 2)),
            dma((8, 2)),
            dma((8, 2)),
            dma((2,)),
            dma((2,)),
            dma((8, 2)),
            dma((8, 2)),
            dma((2, 5, 2)),
            dma((2, 5, 2)),
            dma((7,)),
            dma((7,)),
        ],
        compiler_params=pltpu.CompilerParams(
            collective_id=0, has_side_effects=True, vmem_limit_bytes=48 * 1024 * 1024
        ),
    )(jnp.transpose(residual, (0, 2, 1)), encoder, enc_bias, gate_code, decoder)


def solution(mesh):
    return jax.shard_map(
        shards,
        mesh=mesh,
        in_specs=(
            P(None, None, "latent"),
            P("section", None, "latent"),
            P("section", "latent"),
            P("section", "latent"),
            P("section", None, "latent", None),
        ),
        out_specs=(P("section", None, "latent"), P("section", None, "latent")),
        check_vma=False,
    )
```

```python
import jax
import jax.numpy as jnp
from jax import lax
from jax.experimental import pallas as pl
from jax.experimental.pallas import tpu as pltpu
from jax.sharding import PartitionSpec as P

MESH = pl.DeviceIdType.MESH
BF16 = jnp.bfloat16
F32 = jnp.float32

NY = 8
GROUP = 4
LANES = 128
OFFSETS = (4, 3, -3, 2, -2, 1, -1, 0)
PLACE = {offset: place for place, offset in enumerate(OFFSETS)}
PLACE[-4] = PLACE[4]
TILES = ((0, 1), (2, 3), (4,))
FAR = (0, 1, 0, 1, 0)
FIRST = (0, 128, 256)
COUNT = (128, 128, 64)
PIECES = (
    (0, 0, 0, 80, 0),
    (0, 1, 80, 48, 0),
    (1, 1, 128, 32, 48),
    (1, 2, 160, 80, 0),
    (1, 3, 240, 16, 0),
    (2, 3, 256, 64, 16),
)


def kernel(
    resid, enc, bias, gate, dec, rec_out, act_out,
    resid_v, bias_v, gate_v, last_out, last_in, gathered, enc_v, dec_v, enc_t, dec_t, acts_in, acts_all,
    shares, sibling_in, ring, own_sum, final_out, final_in,
    load_sem, cross_send, cross_recv, gather_send, gather_recv, pair_send, pair_recv,
    act_send, act_recv, share_send, share_recv, ring_send, ring_recv, final_send, final_recv,
):
    width = gathered.shape[3]
    section = lax.axis_index("section")
    latent = lax.axis_index("latent")
    x_lo, z = section // 8, section % 8
    x_hi, y, core = latent // 16, latent // 2 % 8, latent % 2
    layer, g = section // GROUP, section % GROUP
    half = (x_hi, 1 - x_hi)

    def device(section_index, hi, y_index, core_index):
        return (section_index, hi * 16 + y_index * 2 + core_index)

    ways = (device(section, x_hi, (y + 1) % NY, core), device(section, x_hi, (y + NY - 1) % NY, core))
    sibling = device(section, x_hi, y, 1 - core)
    across = device((1 - x_lo) * 8 + z, 1 - x_hi, y, core)
    later = [((section + 4) % 16, latent), ((section + 8) % 16, latent)]
    partners = [*ways, sibling, across, later[0], later[1], ((section + 12) % 16, latent)]
    for turn in range(GROUP):
        for q in range(2):
            if turn or q:
                partners.append(device(section - g + (g + turn) % GROUP, half[q], y, core))
    barrier = pltpu.get_barrier_semaphore()
    for partner in partners:
        pl.semaphore_signal(barrier, inc=1, device_id=partner, device_id_type=MESH)
    loads = [
        pltpu.make_async_copy(resid.at[layer], resid_v.at[0], load_sem.at[0]),
        pltpu.make_async_copy(resid.at[(1 - x_lo) * 2 + z // 4], resid_v.at[1], load_sem.at[1]),
        pltpu.make_async_copy(enc.at[0], enc_v, load_sem.at[2]),
        pltpu.make_async_copy(dec.at[0], dec_v, load_sem.at[3]),
        pltpu.make_async_copy(bias, bias_v, load_sem.at[4]),
        pltpu.make_async_copy(gate, gate_v, load_sem.at[5]),
    ]
    for load in loads:
        load.start()

    def remote(source, target, send, recv, to):
        copy = pltpu.make_async_remote_copy(
            src_ref=source, dst_ref=target, send_sem=send, recv_sem=recv, device_id=to, device_id_type=MESH
        )
        copy.start()
        return copy

    loads[0].wait()
    loads[1].wait()
    for chunk in range(2):
        gathered[2 * chunk + x_hi, y, core] = resid_v[0, :, chunk * LANES : (chunk + 1) * LANES]
    last_out[:, 0:64] = resid_v[1, :, 256:320]
    last_out[:, 64:128] = resid_v[1, :, 256:320]
    pl.semaphore_wait(barrier, len(partners))

    gather, pairs = {}, {}
    units = ((0, 1), (2, 3), (4,))

    def tile_of(unit):
        return 4 if unit == 4 else unit // 2 * 2 + half[unit % 2]

    def around(offset):
        return (y + (offset + NY) % NY) % NY

    def send_gather(step, way, unit):
        block = gathered.at[tile_of(unit), around(-step if way == 0 else step), core]
        gather[step, way, unit] = remote(
            block, block, gather_send.at[step, way, unit], gather_recv.at[step, way, unit], ways[way]
        )

    def send_pair(offset, unit):
        block = gathered.at[tile_of(unit), around(offset), core]
        place = PLACE[offset]
        pairs[place, unit] = remote(block, block, pair_send.at[place, unit], pair_recv.at[place, unit], sibling)

    crossed = []
    for chunk in range(2):
        crossed.append(
            remote(
                resid_v.at[1, :, pl.ds(chunk * LANES, LANES)],
                gathered.at[2 * chunk + x_hi, y, core],
                cross_send.at[chunk],
                cross_recv.at[chunk],
                across,
            )
        )
    crossed.append(remote(last_out, last_in, cross_send.at[2], cross_recv.at[2], across))
    for chunk in range(2):
        for way in range(2):
            send_gather(0, way, 2 * chunk)
        send_pair(0, 2 * chunk)

    loads[2].wait()

    def turn_encoder(block, carry):
        rows = pl.ds(pl.multiple_of(block * 2 * width, 16), 2 * width)
        enc_t[block] = jnp.transpose(enc_v[rows, :])
        return carry

    lax.fori_loop(0, 8, turn_encoder, 0)
    for chunk in range(2):
        crossed[chunk].wait_recv()
        for way in range(2):
            send_gather(0, way, 2 * chunk + 1)
        send_pair(0, 2 * chunk + 1)
    crossed[2].wait_recv()
    own_last, other_last = resid_v[0, :, 256:320], last_in[:, 0:64]
    is_low = x_hi == 0
    gathered[4, y, core] = jnp.concatenate(
        [jnp.where(is_low, own_last, other_last), jnp.where(is_low, other_last, own_last)], axis=1
    )
    for way in range(2):
        send_gather(0, way, 4)
    send_pair(0, 4)
    lax.fori_loop(8, 16, turn_encoder, 0)
    for load in loads[3:]:
        load.wait()

    def turn_decoder(block, carry):
        columns = pl.ds(pl.multiple_of(block * 128, 128), 128)
        for k in range(3):
            dec_t[columns, k * 128 : (k + 1) * 128] = jnp.transpose(dec_v[k, :, columns])
        return carry

    def receive(chunk, step):
        for unit in units[chunk]:
            far = unit % 2
            for way in range(2):
                if (step, way, unit) not in gather:
                    continue
                gather[step, way, unit].wait_recv()
                if step < 2 or (step == 2 and way == far):
                    send_gather(step + 1, way, unit)
                send_pair((step + 1) * (-1 if way == 0 else 1), unit)

    preacts = {}

    def encode(chunk, offset):
        origin = around(offset)
        for unit in units[chunk]:
            pairs[PLACE[offset], unit].wait_recv()
        for hi in range(2):
            block = gathered[TILES[chunk][hi] if chunk < 2 else 4, origin].reshape(2 * width, LANES)
            term = jnp.dot(enc_t[hi * NY + origin], block, preferred_element_type=F32)
            key = (chunk, hi if chunk == 2 else 0)
            preacts[key] = term if key not in preacts else preacts[key] + term

    passed = {}

    def activate(chunk):
        first, count = FIRST[chunk], COUNT[chunk]
        preact = jnp.transpose(preacts[chunk, 0])
        if chunk == 2:
            preact = preact[0:64] + jnp.transpose(preacts[2, 1])[64:128]
        preact = preact + bias_v[...]
        threshold = 10000.0 * (gate_v[...].astype(F32) - 1.0)
        acts = jnp.where(preact > threshold, preact, jnp.zeros_like(preact)).astype(BF16)
        act_out[0, first : first + count] = acts
        rows = pl.ds(first, count)
        for k in range(2):
            passed[chunk, k] = remote(
                act_out.at[0, rows], acts_in.at[k, rows], act_send.at[chunk, k], act_recv.at[chunk, k], later[k]
            )
        fill(chunk, 0, acts)

    def fill(chunk, k, acts):
        first, count = FIRST[chunk], COUNT[chunk]
        acts_all[first : first + count, k * 128 : (k + 1) * 128] = acts
        if chunk == 2:
            acts_all[320:384, k * 128 : (k + 1) * 128] = acts

    def take(chunk):
        first, count = FIRST[chunk], COUNT[chunk]
        for k in range(2):
            passed[chunk, k].wait_recv()
            arrived = acts_in[k, first : first + count]
            fill(chunk, k + 1, jnp.where(layer > k, arrived, jnp.zeros_like(arrived)))

    share_copies, ring_copies = {}, {}

    def decode(chunk, place):
        target = around(OFFSETS[place])

        def product(hi):
            rows = pl.ds(pl.multiple_of((hi * NY + target) * 2 * width, 16), 2 * width)
            return lax.dot_general(
                dec_t[rows, :],
                acts_all[chunk * LANES : (chunk + 1) * LANES],
                (((1,), (1,)), ((), ())),
                preferred_element_type=F32,
            )

        if chunk == 2:
            lane = lax.broadcasted_iota(jnp.int32, (2 * width, LANES), 1)
            shares[place, 4] = jnp.where(lane < 64, product(0), product(1)).astype(BF16).reshape(2, width, LANES)
        else:
            for hi in range(2):
                shares[place, TILES[chunk][hi]] = product(hi).astype(BF16).reshape(2, width, LANES)
        for tile in TILES[chunk]:
            share_copies[place, tile] = remote(
                shares.at[place, tile, 1 - core],
                sibling_in.at[place, tile],
                share_send.at[place, tile],
                share_recv.at[place, tile],
                sibling,
            )

    def chip_sum(place, tile):
        share_copies[place, tile].wait_recv()
        return shares[place, tile, core].astype(F32) + sibling_in[place, tile].astype(F32)

    def add_ring(way, distance, tile):
        total = chip_sum(PLACE[distance if way == 0 else -distance], tile)
        if (way, distance + 1, tile) in ring_copies:
            ring_copies[way, distance + 1, tile].wait_recv()
            total = total + ring[way, distance, tile].astype(F32)
        ring[way, distance, tile] = total.astype(BF16)
        ring_copies[way, distance, tile] = remote(
            ring.at[way, distance, tile],
            ring.at[way, distance - 1, tile],
            ring_send.at[way, distance, tile],
            ring_recv.at[way, distance, tile],
            ways[way],
        )

    def add_far(chunk):
        for tile in TILES[chunk]:
            add_ring(FAR[tile], 4, tile)

    def add_near(chunk):
        for tile in TILES[chunk]:
            add_ring(1 - FAR[tile], 3, tile)

    def add_third(chunk):
        for tile in TILES[chunk]:
            add_ring(FAR[tile], 3, tile)

    def add_both(chunk, distance):
        for tile in TILES[chunk]:
            for way in range(2):
                add_ring(way if tile % 2 else 1 - way, distance, tile)

    always, others = [], []

    def finish(chunk):
        first, count = FIRST[chunk], COUNT[chunk]
        for tile in TILES[chunk]:
            total = chip_sum(7, tile)
            for way in range(2):
                ring_copies[way, 1, tile].wait_recv()
                total = total + ring[way, 0, tile].astype(F32)
            turned = jnp.transpose(total)
            parts = ((0, turned[0:64]), (1, turned[64:128])) if chunk == 2 else ((tile % 2, turned),)
            for hi, part in parts:
                own_sum[hi, first : first + count] = part
                final_out[hi, first : first + count] = part.astype(BF16)
        for index, (piece_chunk, target, token, rows, row) in enumerate(PIECES):
            if piece_chunk != chunk:
                continue

            def copy_to(q, index=index, target=target, token=token, rows=rows, row=row):
                return pltpu.make_async_remote_copy(
                    src_ref=final_out.at[half[q], pl.ds(token, rows)],
                    dst_ref=final_in.at[q * GROUP + g, pl.ds(row, rows)],
                    send_sem=final_send.at[index, q],
                    recv_sem=final_recv.at[index, q * GROUP + g],
                    device_id=device(section - g + target, half[q], y, core),
                    device_id_type=MESH,
                )

            far = copy_to(1)
            far.start()
            always.append(far)
            near = copy_to(0)
            others.append((target, near))

            @pl.when(g != target)
            def _(near=near):
                near.start()

    def collect(index):
        _, target, token, rows, row = PIECES[index]

        @pl.when(g == target)
        def _():
            total = own_sum[x_hi, token : token + rows]
            for q in range(2):
                for source in range(GROUP):
                    if q == 0 and source == target:
                        continue
                    slot = q * GROUP + source
                    arrived = final_in.at[slot, pl.ds(row, rows)]
                    pltpu.make_async_remote_copy(
                        src_ref=arrived,
                        dst_ref=arrived,
                        send_sem=final_send.at[index, q],
                        recv_sem=final_recv.at[index, slot],
                        device_id=device(section - g + source, half[q], y, core),
                        device_id_type=MESH,
                    ).wait_recv()
                    total = total + final_in[slot, row : row + rows].astype(F32)
            rec_out[0, row : row + rows] = total.astype(BF16)

    turned_to = [0]

    def turn_some(count):
        stop = min(36, turned_to[0] + count)
        lax.fori_loop(turned_to[0], stop, turn_decoder, 0)
        turned_to[0] = stop

    turn_some(4)
    receive(0, 0)
    receive(1, 0)
    encode(0, 0)
    encode(1, 0)
    receive(2, 0)
    turn_some(4)
    receive(0, 1)
    receive(1, 1)
    for chunk in range(2):
        encode(chunk, 1)
        encode(chunk, -1)
    receive(2, 1)
    turn_some(8)
    encode(2, 0)
    receive(0, 2)
    encode(0, 2)
    encode(0, -2)
    receive(1, 2)
    encode(1, 2)
    encode(1, -2)
    receive(2, 2)
    turn_some(8)
    encode(0, 3)
    encode(0, -3)
    receive(0, 3)
    encode(1, 3)
    encode(1, -3)
    encode(0, 4)
    activate(0)
    receive(1, 3)
    turn_some(4)
    encode(1, 4)
    activate(1)
    for offset in (1, -1, 2, -2, 3, -3):
        encode(2, offset)
    receive(2, 3)
    encode(2, 4)
    activate(2)
    turn_some(36)

    take(0)
    decode(0, 0)
    decode(0, 1)
    add_far(0)
    decode(0, 2)
    add_near(0)
    decode(0, 3)
    decode(0, 4)
    add_third(0)
    take(1)
    decode(1, 0)
    decode(1, 1)
    add_far(1)
    decode(1, 2)
    add_near(1)
    decode(0, 5)
    decode(0, 6)
    add_both(0, 2)
    decode(1, 3)
    decode(1, 4)
    add_third(1)
    take(2)
    decode(2, 0)
    decode(2, 1)
    add_far(2)
    decode(2, 2)
    add_near(2)
    decode(0, 7)
    add_both(0, 1)
    decode(1, 5)
    decode(1, 6)
    add_both(1, 2)
    decode(2, 3)
    decode(2, 4)
    add_third(2)
    decode(1, 7)
    finish(0)
    add_both(1, 1)
    decode(2, 5)
    decode(2, 6)
    add_both(2, 2)
    decode(2, 7)
    finish(1)
    add_both(2, 1)
    finish(2)
    for index in range(len(PIECES)):
        collect(index)

    for group in (crossed, gather.values(), pairs.values(), passed.values(), share_copies.values(), ring_copies.values(), always):
        for copy in group:
            copy.wait_send()
    for target, near in others:

        @pl.when(g != target)
        def _(near=near):
            near.wait_send()


def shards(residual, encoder, enc_bias, gate_code, decoder):
    layers, tokens, width = residual.shape
    model = encoder.shape[1]
    vmem = pl.BlockSpec(memory_space=pltpu.VMEM)
    hbm = pl.BlockSpec(memory_space=pltpu.HBM)
    dma = pltpu.SemaphoreType.DMA
    return pl.pallas_call(
        kernel,
        out_shape=(
            jax.ShapeDtypeStruct((1, tokens // GROUP, width), BF16),
            jax.ShapeDtypeStruct((1, tokens, 128), BF16),
        ),
        in_specs=[hbm] * 5,
        out_specs=(vmem, vmem),
        scratch_shapes=[
            pltpu.VMEM((2, width, tokens), BF16),
            pltpu.VMEM((1, 128), F32),
            pltpu.VMEM((1, 128), jnp.int32),
            pltpu.VMEM((width, LANES), BF16),
            pltpu.VMEM((width, LANES), BF16),
            pltpu.VMEM((5, NY, 2, width, LANES), BF16),
            pltpu.VMEM((model, 128), BF16),
            pltpu.VMEM((3, 128, model), BF16),
            pltpu.VMEM((16, 128, 2 * width), BF16),
            pltpu.VMEM((model, 384), BF16),
            pltpu.VMEM((2, tokens, 128), BF16),
            pltpu.VMEM((384, 384), BF16),
            pltpu.VMEM((8, 5, 2, width, LANES), BF16),
            pltpu.VMEM((8, 5, width, LANES), BF16),
            pltpu.VMEM((2, 5, 5, width, LANES), BF16),
            pltpu.VMEM((2, tokens, width), F32),
            pltpu.VMEM((2, tokens, width), BF16),
            pltpu.VMEM((8, tokens // GROUP, width), BF16),
            dma((6,)),
            dma((3,)),
            dma((3,)),
            dma((4, 2, 5)),
            dma((4, 2, 5)),
            dma((8, 5)),
            dma((8, 5)),
            dma((3, 2)),
            dma((3, 2)),
            dma((8, 5)),
            dma((8, 5)),
            dma((2, 5, 5)),
            dma((2, 5, 5)),
            dma((len(PIECES), 2)),
            dma((len(PIECES), 2 * GROUP)),
        ],
        compiler_params=pltpu.CompilerParams(
            collective_id=0, has_side_effects=True, vmem_limit_bytes=60 * 1024 * 1024
        ),
    )(jnp.transpose(residual, (0, 2, 1)), encoder, enc_bias, gate_code, decoder)


def solution(mesh):
    return jax.shard_map(
        shards,
        mesh=mesh,
        in_specs=(
            P(None, None, "latent"),
            P("section", None, "latent"),
            P("section", "latent"),
            P("section", "latent"),
            P("section", None, "latent", None),
        ),
        out_specs=(P("section", None, "latent"), P("section", None, "latent")),
        check_vma=False,
    )
```

```python
import jax
import jax.numpy as jnp
from jax import lax
from jax.experimental import pallas as pl
from jax.experimental.pallas import tpu as pltpu
from jax.sharding import PartitionSpec as P

MESH = pl.DeviceIdType.MESH
BF16 = jnp.bfloat16
F32 = jnp.float32

NY = 8
GROUP = 4
LANES = 128
OFFSETS = (4, 3, -3, 2, -2, 1, -1, 0)
PLACE = {offset: place for place, offset in enumerate(OFFSETS)}
PLACE[-4] = PLACE[4]
TILES = ((0, 1), (2, 3), (4,))
FAR = (0, 1, 0, 1, 0)
FIRST = (0, 128, 256)
COUNT = (128, 128, 64)
PIECES = (
    (0, 0, 0, 80, 0),
    (0, 1, 80, 48, 0),
    (1, 1, 128, 32, 48),
    (1, 2, 160, 80, 0),
    (1, 3, 240, 16, 0),
    (2, 3, 256, 64, 16),
)


def kernel(
    resid, enc, bias, gate, dec, rec_out, act_out,
    resid_v, bias_v, gate_v, last_out, last_in, gathered, enc_v, dec_v, enc_t, dec_t, acts_in, acts_all,
    shares, sibling_in, ring, own_sum, final_out, final_in,
    load_sem, cross_send, cross_recv, gather_send, gather_recv, pair_send, pair_recv,
    act_send, act_recv, share_send, share_recv, ring_send, ring_recv, final_send, final_recv,
):
    width = gathered.shape[3]
    section = lax.axis_index("section")
    latent = lax.axis_index("latent")
    x_lo, z = section // 8, section % 8
    x_hi, y, core = latent // 16, latent // 2 % 8, latent % 2
    layer, g = section // GROUP, section % GROUP
    half = (x_hi, 1 - x_hi)

    def device(section_index, hi, y_index, core_index):
        return (section_index, hi * 16 + y_index * 2 + core_index)

    ways = (device(section, x_hi, (y + 1) % NY, core), device(section, x_hi, (y + NY - 1) % NY, core))
    sibling = device(section, x_hi, y, 1 - core)
    across = device((1 - x_lo) * 8 + z, 1 - x_hi, y, core)
    later = [((section + 4) % 16, latent), ((section + 8) % 16, latent)]
    partners = [*ways, sibling, across, later[0], later[1], ((section + 12) % 16, latent)]
    for turn in range(GROUP):
        for q in range(2):
            if turn or q:
                partners.append(device(section - g + (g + turn) % GROUP, half[q], y, core))
    barrier = pltpu.get_barrier_semaphore()
    for partner in partners:
        pl.semaphore_signal(barrier, inc=1, device_id=partner, device_id_type=MESH)
    loads = [
        pltpu.make_async_copy(resid.at[layer], resid_v.at[0], load_sem.at[0]),
        pltpu.make_async_copy(resid.at[(1 - x_lo) * 2 + z // 4], resid_v.at[1], load_sem.at[1]),
        pltpu.make_async_copy(enc.at[0], enc_v, load_sem.at[2]),
        pltpu.make_async_copy(dec.at[0], dec_v, load_sem.at[3]),
        pltpu.make_async_copy(bias, bias_v, load_sem.at[4]),
        pltpu.make_async_copy(gate, gate_v, load_sem.at[5]),
    ]
    for load in loads:
        load.start()

    def remote(source, target, send, recv, to):
        copy = pltpu.make_async_remote_copy(
            src_ref=source, dst_ref=target, send_sem=send, recv_sem=recv, device_id=to, device_id_type=MESH
        )
        copy.start()
        return copy

    loads[0].wait()
    loads[1].wait()
    for chunk in range(2):
        gathered[2 * chunk + x_hi, y, core] = resid_v[0, :, chunk * LANES : (chunk + 1) * LANES]
    last_out[:, 0:64] = resid_v[1, :, 256:320]
    last_out[:, 64:128] = resid_v[1, :, 256:320]
    def turn_encoder(block, carry):
        rows = pl.ds(pl.multiple_of(block * 2 * width, 16), 2 * width)
        enc_t[block] = jnp.transpose(enc_v[rows, :])
        return carry

    loads[2].wait()
    lax.fori_loop(0, 16, turn_encoder, 0)
    for load in loads[3:]:
        load.wait()
    pl.semaphore_wait(barrier, len(partners))

    def turn_decoder(block, carry):
        columns = pl.ds(pl.multiple_of(block * 128, 128), 128)
        for k in range(3):
            dec_t[columns, k * 128 : (k + 1) * 128] = jnp.transpose(dec_v[k, :, columns])
        return carry


    gather, pairs = {}, {}
    units = ((0, 1), (2, 3), (4,))

    def tile_of(unit):
        return 4 if unit == 4 else unit // 2 * 2 + half[unit % 2]

    def around(offset):
        return (y + (offset + NY) % NY) % NY

    def send_gather(step, way, unit):
        block = gathered.at[tile_of(unit), around(-step if way == 0 else step), core]
        gather[step, way, unit] = remote(
            block, block, gather_send.at[step, way, unit], gather_recv.at[step, way, unit], ways[way]
        )

    def send_pair(offset, unit):
        block = gathered.at[tile_of(unit), around(offset), core]
        place = PLACE[offset]
        pairs[place, unit] = remote(block, block, pair_send.at[place, unit], pair_recv.at[place, unit], sibling)

    crossed = []
    for chunk in range(2):
        crossed.append(
            remote(
                resid_v.at[1, :, pl.ds(chunk * LANES, LANES)],
                gathered.at[2 * chunk + x_hi, y, core],
                cross_send.at[chunk],
                cross_recv.at[chunk],
                across,
            )
        )
    crossed.append(remote(last_out, last_in, cross_send.at[2], cross_recv.at[2], across))
    for chunk in range(2):
        for way in range(2):
            send_gather(0, way, 2 * chunk)
        send_pair(0, 2 * chunk)

    for chunk in range(2):
        crossed[chunk].wait_recv()
        for way in range(2):
            send_gather(0, way, 2 * chunk + 1)
        send_pair(0, 2 * chunk + 1)
    crossed[2].wait_recv()
    own_last, other_last = resid_v[0, :, 256:320], last_in[:, 0:64]
    is_low = x_hi == 0
    gathered[4, y, core] = jnp.concatenate(
        [jnp.where(is_low, own_last, other_last), jnp.where(is_low, other_last, own_last)], axis=1
    )
    for way in range(2):
        send_gather(0, way, 4)
    send_pair(0, 4)

    def receive(chunk, step):
        for unit in units[chunk]:
            far = unit % 2
            for way in range(2):
                if (step, way, unit) not in gather:
                    continue
                gather[step, way, unit].wait_recv()
                if step < 2 or (step == 2 and way == far):
                    send_gather(step + 1, way, unit)
                send_pair((step + 1) * (-1 if way == 0 else 1), unit)

    preacts = {}

    def encode(chunk, offset):
        origin = around(offset)
        for unit in units[chunk]:
            pairs[PLACE[offset], unit].wait_recv()
        for hi in range(2):
            block = gathered[TILES[chunk][hi] if chunk < 2 else 4, origin].reshape(2 * width, LANES)
            term = jnp.dot(enc_t[hi * NY + origin], block, preferred_element_type=F32)
            key = (chunk, hi if chunk == 2 else 0)
            preacts[key] = term if key not in preacts else preacts[key] + term

    passed = {}

    def activate(chunk):
        first, count = FIRST[chunk], COUNT[chunk]
        preact = jnp.transpose(preacts[chunk, 0])
        if chunk == 2:
            preact = preact[0:64] + jnp.transpose(preacts[2, 1])[64:128]
        preact = preact + bias_v[...]
        threshold = 10000.0 * (gate_v[...].astype(F32) - 1.0)
        acts = jnp.where(preact > threshold, preact, jnp.zeros_like(preact)).astype(BF16)
        act_out[0, first : first + count] = acts
        rows = pl.ds(first, count)
        for k in range(2):
            passed[chunk, k] = remote(
                act_out.at[0, rows], acts_in.at[k, rows], act_send.at[chunk, k], act_recv.at[chunk, k], later[k]
            )
        fill(chunk, 0, acts)

    def fill(chunk, k, acts):
        first, count = FIRST[chunk], COUNT[chunk]
        acts_all[first : first + count, k * 128 : (k + 1) * 128] = acts
        if chunk == 2:
            acts_all[320:384, k * 128 : (k + 1) * 128] = acts

    def take(chunk):
        first, count = FIRST[chunk], COUNT[chunk]
        for k in range(2):
            passed[chunk, k].wait_recv()
            arrived = acts_in[k, first : first + count]
            fill(chunk, k + 1, jnp.where(layer > k, arrived, jnp.zeros_like(arrived)))

    share_copies, ring_copies = {}, {}

    def decode(chunk, place):
        target = around(OFFSETS[place])

        def product(hi):
            rows = pl.ds(pl.multiple_of((hi * NY + target) * 2 * width, 16), 2 * width)
            return lax.dot_general(
                dec_t[rows, :],
                acts_all[chunk * LANES : (chunk + 1) * LANES],
                (((1,), (1,)), ((), ())),
                preferred_element_type=F32,
            )

        if chunk == 2:
            lane = lax.broadcasted_iota(jnp.int32, (2 * width, LANES), 1)
            shares[place, 4] = jnp.where(lane < 64, product(0), product(1)).astype(BF16).reshape(2, width, LANES)
        else:
            for hi in range(2):
                shares[place, TILES[chunk][hi]] = product(hi).astype(BF16).reshape(2, width, LANES)
        for tile in TILES[chunk]:
            share_copies[place, tile] = remote(
                shares.at[place, tile, 1 - core],
                sibling_in.at[place, tile],
                share_send.at[place, tile],
                share_recv.at[place, tile],
                sibling,
            )

    def chip_sum(place, tile):
        share_copies[place, tile].wait_recv()
        return shares[place, tile, core].astype(F32) + sibling_in[place, tile].astype(F32)

    def add_ring(way, distance, tile):
        total = chip_sum(PLACE[distance if way == 0 else -distance], tile)
        if (way, distance + 1, tile) in ring_copies:
            ring_copies[way, distance + 1, tile].wait_recv()
            total = total + ring[way, distance, tile].astype(F32)
        ring[way, distance, tile] = total.astype(BF16)
        ring_copies[way, distance, tile] = remote(
            ring.at[way, distance, tile],
            ring.at[way, distance - 1, tile],
            ring_send.at[way, distance, tile],
            ring_recv.at[way, distance, tile],
            ways[way],
        )

    def add_far(chunk):
        for tile in TILES[chunk]:
            add_ring(FAR[tile], 4, tile)

    def add_near(chunk):
        for tile in TILES[chunk]:
            add_ring(1 - FAR[tile], 3, tile)

    def add_third(chunk):
        for tile in TILES[chunk]:
            add_ring(FAR[tile], 3, tile)

    def add_both(chunk, distance):
        for tile in TILES[chunk]:
            for way in range(2):
                add_ring(way if tile % 2 else 1 - way, distance, tile)

    always, others = [], []

    def finish(chunk):
        first, count = FIRST[chunk], COUNT[chunk]
        for tile in TILES[chunk]:
            total = chip_sum(7, tile)
            for way in range(2):
                ring_copies[way, 1, tile].wait_recv()
                total = total + ring[way, 0, tile].astype(F32)
            turned = jnp.transpose(total)
            parts = ((0, turned[0:64]), (1, turned[64:128])) if chunk == 2 else ((tile % 2, turned),)
            for hi, part in parts:
                own_sum[hi, first : first + count] = part
                final_out[hi, first : first + count] = part.astype(BF16)
        for index, (piece_chunk, target, token, rows, row) in enumerate(PIECES):
            if piece_chunk != chunk:
                continue

            def copy_to(q, index=index, target=target, token=token, rows=rows, row=row):
                return pltpu.make_async_remote_copy(
                    src_ref=final_out.at[half[q], pl.ds(token, rows)],
                    dst_ref=final_in.at[q * GROUP + g, pl.ds(row, rows)],
                    send_sem=final_send.at[index, q],
                    recv_sem=final_recv.at[index, q * GROUP + g],
                    device_id=device(section - g + target, half[q], y, core),
                    device_id_type=MESH,
                )

            far = copy_to(1)
            far.start()
            always.append(far)
            near = copy_to(0)
            others.append((target, near))

            @pl.when(g != target)
            def _(near=near):
                near.start()

    def collect(index):
        _, target, token, rows, row = PIECES[index]

        @pl.when(g == target)
        def _():
            total = own_sum[x_hi, token : token + rows]
            for q in range(2):
                for source in range(GROUP):
                    if q == 0 and source == target:
                        continue
                    slot = q * GROUP + source
                    arrived = final_in.at[slot, pl.ds(row, rows)]
                    pltpu.make_async_remote_copy(
                        src_ref=arrived,
                        dst_ref=arrived,
                        send_sem=final_send.at[index, q],
                        recv_sem=final_recv.at[index, slot],
                        device_id=device(section - g + source, half[q], y, core),
                        device_id_type=MESH,
                    ).wait_recv()
                    total = total + final_in[slot, row : row + rows].astype(F32)
            rec_out[0, row : row + rows] = total.astype(BF16)

    turned_to = [0]

    def turn_some(count):
        stop = min(36, turned_to[0] + count)
        lax.fori_loop(turned_to[0], stop, turn_decoder, 0)
        turned_to[0] = stop

    turn_some(4)
    receive(0, 0)
    receive(1, 0)
    encode(0, 0)
    encode(1, 0)
    receive(2, 0)
    turn_some(4)
    receive(0, 1)
    receive(1, 1)
    for chunk in range(2):
        encode(chunk, 1)
        encode(chunk, -1)
    receive(2, 1)
    turn_some(8)
    encode(2, 0)
    receive(0, 2)
    encode(0, 2)
    encode(0, -2)
    receive(1, 2)
    encode(1, 2)
    encode(1, -2)
    receive(2, 2)
    turn_some(8)
    encode(0, 3)
    encode(0, -3)
    receive(0, 3)
    encode(1, 3)
    encode(1, -3)
    encode(0, 4)
    activate(0)
    receive(1, 3)
    turn_some(4)
    encode(1, 4)
    activate(1)
    for offset in (1, -1, 2, -2, 3, -3):
        encode(2, offset)
    receive(2, 3)
    encode(2, 4)
    activate(2)
    turn_some(36)

    take(0)
    decode(0, 0)
    decode(0, 1)
    add_far(0)
    decode(0, 2)
    add_near(0)
    decode(0, 3)
    decode(0, 4)
    add_third(0)
    take(1)
    decode(1, 0)
    decode(1, 1)
    add_far(1)
    decode(1, 2)
    add_near(1)
    decode(0, 5)
    decode(0, 6)
    add_both(0, 2)
    decode(1, 3)
    decode(1, 4)
    add_third(1)
    take(2)
    decode(2, 0)
    decode(2, 1)
    add_far(2)
    decode(2, 2)
    add_near(2)
    decode(0, 7)
    add_both(0, 1)
    decode(1, 5)
    decode(1, 6)
    add_both(1, 2)
    decode(2, 3)
    decode(2, 4)
    add_third(2)
    decode(1, 7)
    finish(0)
    add_both(1, 1)
    decode(2, 5)
    decode(2, 6)
    add_both(2, 2)
    decode(2, 7)
    finish(1)
    add_both(2, 1)
    finish(2)
    for index in range(len(PIECES)):
        collect(index)

    for group in (crossed, gather.values(), pairs.values(), passed.values(), share_copies.values(), ring_copies.values(), always):
        for copy in group:
            copy.wait_send()
    for target, near in others:

        @pl.when(g != target)
        def _(near=near):
            near.wait_send()


def hand_over(sums, acts, turned, copied):
    turned[0] = jnp.transpose(sums[0])
    copied[...] = acts[...]


def shards(residual, encoder, enc_bias, gate_code, decoder):
    layers, tokens, width = residual.shape
    model = encoder.shape[1]
    vmem = pl.BlockSpec(memory_space=pltpu.VMEM)
    hbm = pl.BlockSpec(memory_space=pltpu.HBM)
    dma = pltpu.SemaphoreType.DMA
    sums, acts = pl.pallas_call(
        kernel,
        out_shape=(
            jax.ShapeDtypeStruct((1, tokens // GROUP, width), BF16),
            jax.ShapeDtypeStruct((1, tokens, 128), BF16),
        ),
        in_specs=[hbm] * 5,
        out_specs=(vmem, vmem),
        scratch_shapes=[
            pltpu.VMEM((2, width, tokens), BF16),
            pltpu.VMEM((1, 128), F32),
            pltpu.VMEM((1, 128), jnp.int32),
            pltpu.VMEM((width, LANES), BF16),
            pltpu.VMEM((width, LANES), BF16),
            pltpu.VMEM((5, NY, 2, width, LANES), BF16),
            pltpu.VMEM((model, 128), BF16),
            pltpu.VMEM((3, 128, model), BF16),
            pltpu.VMEM((16, 128, 2 * width), BF16),
            pltpu.VMEM((model, 384), BF16),
            pltpu.VMEM((2, tokens, 128), BF16),
            pltpu.VMEM((384, 384), BF16),
            pltpu.VMEM((8, 5, 2, width, LANES), BF16),
            pltpu.VMEM((8, 5, width, LANES), BF16),
            pltpu.VMEM((2, 5, 5, width, LANES), BF16),
            pltpu.VMEM((2, tokens, width), F32),
            pltpu.VMEM((2, tokens, width), BF16),
            pltpu.VMEM((8, tokens // GROUP, width), BF16),
            dma((6,)),
            dma((3,)),
            dma((3,)),
            dma((4, 2, 5)),
            dma((4, 2, 5)),
            dma((8, 5)),
            dma((8, 5)),
            dma((3, 2)),
            dma((3, 2)),
            dma((8, 5)),
            dma((8, 5)),
            dma((2, 5, 5)),
            dma((2, 5, 5)),
            dma((len(PIECES), 2)),
            dma((len(PIECES), 2 * GROUP)),
        ],
        compiler_params=pltpu.CompilerParams(
            collective_id=0, has_side_effects=True, vmem_limit_bytes=60 * 1024 * 1024
        ),
    )(jnp.transpose(residual, (0, 2, 1)), encoder, enc_bias, gate_code, decoder)
    turned, copied = pl.pallas_call(
        hand_over,
        out_shape=(
            jax.ShapeDtypeStruct((1, width, tokens // GROUP), BF16),
            jax.ShapeDtypeStruct((1, tokens, 128), BF16),
        ),
        in_specs=[vmem, vmem],
        out_specs=(vmem, vmem),
    )(sums, acts)
    return jnp.transpose(turned, (0, 2, 1)), copied


def solution(mesh):
    return jax.shard_map(
        shards,
        mesh=mesh,
        in_specs=(
            P(None, None, "latent"),
            P("section", None, "latent"),
            P("section", "latent"),
            P("section", "latent"),
            P("section", None, "latent", None),
        ),
        out_specs=(P("section", None, "latent"), P("section", None, "latent")),
        check_vma=False,
    )
```

```python
import jax
import jax.numpy as jnp
from jax import lax
from jax.experimental import pallas as pl
from jax.experimental.pallas import tpu as pltpu
from jax.sharding import PartitionSpec as P

MESH = pl.DeviceIdType.MESH
BF16 = jnp.bfloat16
F32 = jnp.float32

NY = 8
GROUP = 4
LANES = 128
OFFSETS = (4, 3, -3, 2, -2, 1, -1, 0)
PLACE = {offset: place for place, offset in enumerate(OFFSETS)}
PLACE[-4] = PLACE[4]
TILES = ((0, 1), (2, 3), (4,))
FAR = (0, 1, 0, 1, 0)
FIRST = (0, 128, 256)
COUNT = (128, 128, 64)
PIECES = (
    (0, 0, 0, 80, 0),
    (0, 1, 80, 48, 0),
    (1, 1, 128, 32, 48),
    (1, 2, 160, 80, 0),
    (1, 3, 240, 16, 0),
    (2, 3, 256, 64, 16),
)


def kernel(
    resid, enc, bias, gate, dec, rec_out, act_out,
    resid_v, bias_v, gate_v, last_out, last_in, gathered, enc_v, dec_v, enc_t, dec_t, acts_in, acts_all,
    shares, sibling_in, ring, own_sum, final_out, final_in,
    load_sem, cross_send, cross_recv, gather_send, gather_recv, pair_send, pair_recv,
    act_send, act_recv, share_send, share_recv, ring_send, ring_recv, final_send, final_recv,
):
    width = gathered.shape[3]
    section = lax.axis_index("section")
    latent = lax.axis_index("latent")
    x_lo, z = section // 8, section % 8
    x_hi, y, core = latent // 16, latent // 2 % 8, latent % 2
    layer, g = section // GROUP, section % GROUP
    half = (x_hi, 1 - x_hi)

    def device(section_index, hi, y_index, core_index):
        return (section_index, hi * 16 + y_index * 2 + core_index)

    ways = (device(section, x_hi, (y + 1) % NY, core), device(section, x_hi, (y + NY - 1) % NY, core))
    sibling = device(section, x_hi, y, 1 - core)
    across = device((1 - x_lo) * 8 + z, 1 - x_hi, y, core)
    later = [((section + 4) % 16, latent), ((section + 8) % 16, latent)]
    partners = [*ways, sibling, across, later[0], later[1], ((section + 12) % 16, latent)]
    for turn in range(GROUP):
        for q in range(2):
            if turn or q:
                partners.append(device(section - g + (g + turn) % GROUP, half[q], y, core))
    barrier = pltpu.get_barrier_semaphore()
    for partner in partners:
        pl.semaphore_signal(barrier, inc=1, device_id=partner, device_id_type=MESH)
    loads = [
        pltpu.make_async_copy(resid.at[layer], resid_v.at[0], load_sem.at[0]),
        pltpu.make_async_copy(resid.at[(1 - x_lo) * 2 + z // 4], resid_v.at[1], load_sem.at[1]),
        pltpu.make_async_copy(enc.at[0], enc_v, load_sem.at[2]),
        pltpu.make_async_copy(dec.at[0], dec_v, load_sem.at[3]),
        pltpu.make_async_copy(bias, bias_v, load_sem.at[4]),
        pltpu.make_async_copy(gate, gate_v, load_sem.at[5]),
    ]
    for load in loads:
        load.start()

    def remote(source, target, send, recv, to):
        copy = pltpu.make_async_remote_copy(
            src_ref=source, dst_ref=target, send_sem=send, recv_sem=recv, device_id=to, device_id_type=MESH
        )
        copy.start()
        return copy

    loads[0].wait()
    loads[1].wait()
    for chunk in range(2):
        gathered[2 * chunk + x_hi, y, core] = resid_v[0, :, chunk * LANES : (chunk + 1) * LANES]
    last_out[:, 0:64] = resid_v[1, :, 256:320]
    last_out[:, 64:128] = resid_v[1, :, 256:320]
    def turn_encoder(block, carry):
        rows = pl.ds(pl.multiple_of(block * 2 * width, 16), 2 * width)
        enc_t[block] = jnp.transpose(enc_v[rows, :])
        return carry

    loads[2].wait()
    lax.fori_loop(0, 16, turn_encoder, 0)
    for load in loads[3:]:
        load.wait()
    pl.semaphore_wait(barrier, len(partners))

    def turn_decoder(block, carry):
        columns = pl.ds(pl.multiple_of(block * 128, 128), 128)
        for k in range(3):
            dec_t[columns, k * 128 : (k + 1) * 128] = jnp.transpose(dec_v[k, :, columns])
        return carry


    gather, pairs = {}, {}
    units = ((0, 1), (2, 3), (4,))

    def tile_of(unit):
        return 4 if unit == 4 else unit // 2 * 2 + half[unit % 2]

    def around(offset):
        return (y + (offset + NY) % NY) % NY

    def send_gather(step, way, unit):
        block = gathered.at[tile_of(unit), around(-step if way == 0 else step), core]
        gather[step, way, unit] = remote(
            block, block, gather_send.at[step, way, unit], gather_recv.at[step, way, unit], ways[way]
        )

    def send_pair(offset, unit):
        block = gathered.at[tile_of(unit), around(offset), core]
        place = PLACE[offset]
        pairs[place, unit] = remote(block, block, pair_send.at[place, unit], pair_recv.at[place, unit], sibling)

    crossed = []
    for chunk in range(2):
        crossed.append(
            remote(
                resid_v.at[1, :, pl.ds(chunk * LANES, LANES)],
                gathered.at[2 * chunk + x_hi, y, core],
                cross_send.at[chunk],
                cross_recv.at[chunk],
                across,
            )
        )
    crossed.append(remote(last_out, last_in, cross_send.at[2], cross_recv.at[2], across))
    for chunk in range(2):
        for way in range(2):
            send_gather(0, way, 2 * chunk)
        send_pair(0, 2 * chunk)

    for chunk in range(2):
        crossed[chunk].wait_recv()
        for way in range(2):
            send_gather(0, way, 2 * chunk + 1)
        send_pair(0, 2 * chunk + 1)
    crossed[2].wait_recv()
    own_last, other_last = resid_v[0, :, 256:320], last_in[:, 0:64]
    is_low = x_hi == 0
    gathered[4, y, core] = jnp.concatenate(
        [jnp.where(is_low, own_last, other_last), jnp.where(is_low, other_last, own_last)], axis=1
    )
    for way in range(2):
        send_gather(0, way, 4)
    send_pair(0, 4)

    def receive(chunk, step):
        for unit in units[chunk]:
            far = unit % 2
            for way in range(2):
                if (step, way, unit) not in gather:
                    continue
                gather[step, way, unit].wait_recv()
                if step < 2 or (step == 2 and way == far):
                    send_gather(step + 1, way, unit)
                send_pair((step + 1) * (-1 if way == 0 else 1), unit)

    preacts = {}

    def encode(chunk, offset):
        origin = around(offset)
        for unit in units[chunk]:
            pairs[PLACE[offset], unit].wait_recv()
        for hi in range(2):
            block = gathered[TILES[chunk][hi] if chunk < 2 else 4, origin].reshape(2 * width, LANES)
            term = jnp.dot(enc_t[hi * NY + origin], block, preferred_element_type=F32)
            key = (chunk, hi if chunk == 2 else 0)
            preacts[key] = term if key not in preacts else preacts[key] + term

    passed = {}

    def activate(chunk):
        first, count = FIRST[chunk], COUNT[chunk]
        preact = jnp.transpose(preacts[chunk, 0])
        if chunk == 2:
            preact = preact[0:64] + jnp.transpose(preacts[2, 1])[64:128]
        preact = preact + bias_v[...]
        threshold = 10000.0 * (gate_v[...].astype(F32) - 1.0)
        acts = jnp.where(preact > threshold, preact, jnp.zeros_like(preact)).astype(BF16)
        act_out[0, first : first + count] = acts
        rows = pl.ds(first, count)
        for k in range(2):
            passed[chunk, k] = remote(
                act_out.at[0, rows], acts_in.at[k, rows], act_send.at[chunk, k], act_recv.at[chunk, k], later[k]
            )
        fill(chunk, 0, acts)

    def fill(chunk, k, acts):
        first, count = FIRST[chunk], COUNT[chunk]
        acts_all[first : first + count, k * 128 : (k + 1) * 128] = acts
        if chunk == 2:
            acts_all[320:384, k * 128 : (k + 1) * 128] = acts

    def take(chunk):
        first, count = FIRST[chunk], COUNT[chunk]
        for k in range(2):
            passed[chunk, k].wait_recv()
            arrived = acts_in[k, first : first + count]
            fill(chunk, k + 1, jnp.where(layer > k, arrived, jnp.zeros_like(arrived)))

    share_copies, ring_copies = {}, {}

    def decode(chunk, place):
        target = around(OFFSETS[place])

        def product(hi):
            rows = pl.ds(pl.multiple_of((hi * NY + target) * 2 * width, 16), 2 * width)
            return lax.dot_general(
                dec_t[rows, :],
                acts_all[chunk * LANES : (chunk + 1) * LANES],
                (((1,), (1,)), ((), ())),
                preferred_element_type=F32,
            )

        if chunk == 2:
            lane = lax.broadcasted_iota(jnp.int32, (2 * width, LANES), 1)
            shares[place, 4] = jnp.where(lane < 64, product(0), product(1)).astype(BF16).reshape(2, width, LANES)
        else:
            for hi in range(2):
                shares[place, TILES[chunk][hi]] = product(hi).astype(BF16).reshape(2, width, LANES)
        for tile in TILES[chunk]:
            share_copies[place, tile] = remote(
                shares.at[place, tile, 1 - core],
                sibling_in.at[place, tile],
                share_send.at[place, tile],
                share_recv.at[place, tile],
                sibling,
            )

    def chip_sum(place, tile):
        share_copies[place, tile].wait_recv()
        return shares[place, tile, core].astype(F32) + sibling_in[place, tile].astype(F32)

    def add_ring(way, distance, tile):
        total = chip_sum(PLACE[distance if way == 0 else -distance], tile)
        if (way, distance + 1, tile) in ring_copies:
            ring_copies[way, distance + 1, tile].wait_recv()
            total = total + ring[way, distance, tile].astype(F32)
        ring[way, distance, tile] = total.astype(BF16)
        ring_copies[way, distance, tile] = remote(
            ring.at[way, distance, tile],
            ring.at[way, distance - 1, tile],
            ring_send.at[way, distance, tile],
            ring_recv.at[way, distance, tile],
            ways[way],
        )

    def add_far(chunk):
        for tile in TILES[chunk]:
            add_ring(FAR[tile], 4, tile)

    def add_near(chunk):
        for tile in TILES[chunk]:
            add_ring(1 - FAR[tile], 3, tile)

    def add_third(chunk):
        for tile in TILES[chunk]:
            add_ring(FAR[tile], 3, tile)

    def add_both(chunk, distance):
        for tile in TILES[chunk]:
            for way in range(2):
                add_ring(way if tile % 2 else 1 - way, distance, tile)

    always, others = [], []

    def finish(chunk):
        first, count = FIRST[chunk], COUNT[chunk]
        for tile in TILES[chunk]:
            total = chip_sum(7, tile)
            for way in range(2):
                ring_copies[way, 1, tile].wait_recv()
                total = total + ring[way, 0, tile].astype(F32)
            turned = jnp.transpose(total)
            parts = ((0, turned[0:64]), (1, turned[64:128])) if chunk == 2 else ((tile % 2, turned),)
            for hi, part in parts:
                own_sum[hi, first : first + count] = part
                final_out[hi, first : first + count] = part.astype(BF16)
        for index, (piece_chunk, target, token, rows, row) in enumerate(PIECES):
            if piece_chunk != chunk:
                continue

            def copy_to(q, index=index, target=target, token=token, rows=rows, row=row):
                return pltpu.make_async_remote_copy(
                    src_ref=final_out.at[half[q], pl.ds(token, rows)],
                    dst_ref=final_in.at[q * GROUP + g, pl.ds(row, rows)],
                    send_sem=final_send.at[index, q],
                    recv_sem=final_recv.at[index, q * GROUP + g],
                    device_id=device(section - g + target, half[q], y, core),
                    device_id_type=MESH,
                )

            far = copy_to(1)
            far.start()
            always.append(far)
            near = copy_to(0)
            others.append((target, near))

            @pl.when(g != target)
            def _(near=near):
                near.start()

    def collect(index):
        _, target, token, rows, row = PIECES[index]

        @pl.when(g == target)
        def _():
            total = own_sum[x_hi, token : token + rows]
            for q in range(2):
                for source in range(GROUP):
                    if q == 0 and source == target:
                        continue
                    slot = q * GROUP + source
                    arrived = final_in.at[slot, pl.ds(row, rows)]
                    pltpu.make_async_remote_copy(
                        src_ref=arrived,
                        dst_ref=arrived,
                        send_sem=final_send.at[index, q],
                        recv_sem=final_recv.at[index, slot],
                        device_id=device(section - g + source, half[q], y, core),
                        device_id_type=MESH,
                    ).wait_recv()
                    total = total + final_in[slot, row : row + rows].astype(F32)
            rec_out[0, row : row + rows] = total.astype(BF16)

    turned_to = [0]

    def turn_some(count):
        stop = min(36, turned_to[0] + count)
        lax.fori_loop(turned_to[0], stop, turn_decoder, 0)
        turned_to[0] = stop

    turn_some(4)
    receive(0, 0)
    receive(1, 0)
    encode(0, 0)
    encode(1, 0)
    receive(2, 0)
    turn_some(4)
    receive(0, 1)
    receive(1, 1)
    for chunk in range(2):
        encode(chunk, 1)
        encode(chunk, -1)
    receive(2, 1)
    turn_some(8)
    encode(2, 0)
    receive(0, 2)
    encode(0, 2)
    encode(0, -2)
    receive(1, 2)
    encode(1, 2)
    encode(1, -2)
    receive(2, 2)
    turn_some(8)
    encode(0, 3)
    encode(0, -3)
    receive(0, 3)
    encode(1, 3)
    encode(1, -3)
    encode(0, 4)
    activate(0)
    receive(1, 3)
    turn_some(4)
    encode(1, 4)
    activate(1)
    for offset in (1, -1, 2, -2, 3, -3):
        encode(2, offset)
    receive(2, 3)
    encode(2, 4)
    activate(2)
    turn_some(36)

    take(0)
    decode(0, 0)
    decode(0, 1)
    add_far(0)
    decode(0, 2)
    add_near(0)
    decode(0, 3)
    decode(0, 4)
    add_third(0)
    decode(0, 5)
    decode(0, 6)
    take(1)
    decode(1, 0)
    decode(1, 1)
    add_far(1)
    add_both(0, 2)
    decode(1, 2)
    add_near(1)
    decode(1, 3)
    decode(1, 4)
    add_third(1)
    take(2)
    decode(2, 0)
    decode(2, 1)
    add_far(2)
    decode(2, 2)
    add_near(2)
    decode(0, 7)
    add_both(0, 1)
    decode(1, 5)
    decode(1, 6)
    add_both(1, 2)
    decode(2, 3)
    decode(2, 4)
    add_third(2)
    decode(1, 7)
    finish(0)
    add_both(1, 1)
    decode(2, 5)
    decode(2, 6)
    add_both(2, 2)
    decode(2, 7)
    finish(1)
    add_both(2, 1)
    finish(2)
    for index in range(len(PIECES)):
        collect(index)

    for group in (crossed, gather.values(), pairs.values(), passed.values(), share_copies.values(), ring_copies.values(), always):
        for copy in group:
            copy.wait_send()
    for target, near in others:

        @pl.when(g != target)
        def _(near=near):
            near.wait_send()


def hand_over(sums, acts, turned, copied):
    turned[0] = jnp.transpose(sums[0])
    copied[...] = acts[...]


def shards(residual, encoder, enc_bias, gate_code, decoder):
    layers, tokens, width = residual.shape
    model = encoder.shape[1]
    vmem = pl.BlockSpec(memory_space=pltpu.VMEM)
    hbm = pl.BlockSpec(memory_space=pltpu.HBM)
    dma = pltpu.SemaphoreType.DMA
    sums, acts = pl.pallas_call(
        kernel,
        out_shape=(
            jax.ShapeDtypeStruct((1, tokens // GROUP, width), BF16),
            jax.ShapeDtypeStruct((1, tokens, 128), BF16),
        ),
        in_specs=[hbm] * 5,
        out_specs=(vmem, vmem),
        scratch_shapes=[
            pltpu.VMEM((2, width, tokens), BF16),
            pltpu.VMEM((1, 128), F32),
            pltpu.VMEM((1, 128), jnp.int32),
            pltpu.VMEM((width, LANES), BF16),
            pltpu.VMEM((width, LANES), BF16),
            pltpu.VMEM((5, NY, 2, width, LANES), BF16),
            pltpu.VMEM((model, 128), BF16),
            pltpu.VMEM((3, 128, model), BF16),
            pltpu.VMEM((16, 128, 2 * width), BF16),
            pltpu.VMEM((model, 384), BF16),
            pltpu.VMEM((2, tokens, 128), BF16),
            pltpu.VMEM((384, 384), BF16),
            pltpu.VMEM((8, 5, 2, width, LANES), BF16),
            pltpu.VMEM((8, 5, width, LANES), BF16),
            pltpu.VMEM((2, 5, 5, width, LANES), BF16),
            pltpu.VMEM((2, tokens, width), F32),
            pltpu.VMEM((2, tokens, width), BF16),
            pltpu.VMEM((8, tokens // GROUP, width), BF16),
            dma((6,)),
            dma((3,)),
            dma((3,)),
            dma((4, 2, 5)),
            dma((4, 2, 5)),
            dma((8, 5)),
            dma((8, 5)),
            dma((3, 2)),
            dma((3, 2)),
            dma((8, 5)),
            dma((8, 5)),
            dma((2, 5, 5)),
            dma((2, 5, 5)),
            dma((len(PIECES), 2)),
            dma((len(PIECES), 2 * GROUP)),
        ],
        compiler_params=pltpu.CompilerParams(
            collective_id=0, has_side_effects=True, vmem_limit_bytes=60 * 1024 * 1024
        ),
    )(jnp.transpose(residual, (0, 2, 1)), encoder, enc_bias, gate_code, decoder)
    turned, copied = pl.pallas_call(
        hand_over,
        out_shape=(
            jax.ShapeDtypeStruct((1, width, tokens // GROUP), BF16),
            jax.ShapeDtypeStruct((1, tokens, 128), BF16),
        ),
        in_specs=[vmem, vmem],
        out_specs=(vmem, vmem),
    )(sums, acts)
    return jnp.transpose(turned, (0, 2, 1)), copied


def solution(mesh):
    return jax.shard_map(
        shards,
        mesh=mesh,
        in_specs=(
            P(None, None, "latent"),
            P("section", None, "latent"),
            P("section", "latent"),
            P("section", "latent"),
            P("section", None, "latent", None),
        ),
        out_specs=(P("section", None, "latent"), P("section", None, "latent")),
        check_vma=False,
    )
```
